32 devices in a mesh: rep: 1, fsdp: 32 (over z, y, x, core).
Axes of the slice: x: 2, y: 2, z: 4, core: 2. Of those that a mesh axis runs over, the one named last changes fastest.
Arguments:
- tokens: bfloat16 [24576, 4096], P(('rep', 'fsdp')), may hold values from -6 to 6
- cotangent: bfloat16 [24576, 512], P(('rep', 'fsdp')), may hold values from -0.0390625 to 0.0390625
- policy: float32 [4096, 512], P('fsdp'), may hold values from -0.09375 to 0.09375
- anchor: float32 [4096, 512], P('fsdp'), may hold values from -0.09375 to 0.09375
- moment: float32 [4096, 512], P('fsdp'), may hold values from -3 to 3
- second: float32 [4096, 512], P('fsdp'), may hold values from 0.25 to 4
- readout: float32 [512], replicated, may hold values from -6 to 6
- pair_index: int32 [64, 2], P(('rep', 'fsdp')), may hold values from 0 to 127, as said below
- noisy_flags: int32 [64], P(('rep', 'fsdp')), may hold values 0 or 1
Outputs:
- policy_next: float32 [4096, 512], P('fsdp')
- anchor_next: float32 [4096, 512], P('fsdp')
- moment_next: float32 [4096, 512], P('fsdp')
- second_next: float32 [4096, 512], P('fsdp')
- pair_loss: float32 [64], P(('rep', 'fsdp'))
The draws below stay inside these ranges and needn't reach their ends.
Inputs may be any that keep to these rules, and one draw needn't show every extreme that they name: Each of the 128 sequences appears exactly once in pair_index.
All inputs are finite; a program needn't handle non-finite values. No bound on the sum of `noisy_flags` on one device may be relied on, other than what follows from the above.
Results may differ from the reference program's by a relative error of at most 0.0025.
Values may be sent and summed in bfloat16 or wider, within the bound.
A program may use at most 64 MiB of HBM per device.

```python
import math
import jax
import jax.numpy as jnp
from jax import lax

D = 4096
DV = 512
LEN = 192
TOKENS = 24576
NSEQ = 128
PAIRS = 64


def draw_pair_index(key, part):
    shuffled = jax.random.permutation(jax.random.fold_in(key, 11), NSEQ)
    return shuffled.astype(jnp.int32).reshape(PAIRS, 2)


def touch_ends(values, own_key, least, high):
    longest = values.shape.index(max(values.shape))
    spots = []
    for shift in (0, 1):
        where = [jax.random.randint(jax.random.fold_in(own_key, axis), (), 0, length) for axis, length in enumerate(values.shape)]
        where[longest] = (where[longest] + shift) % values.shape[longest]
        spots.append(tuple(where))
    return values.at[spots[0]].set(least).at[spots[1]].set(high)


def strengthened(entries, rng, source, target, parts, factor):
    owner, partner = [(jnp.arange(entries.shape[position]) // (entries.shape[position] // parts)).reshape([-1 if axis == position else 1 for axis in range(entries.ndim)]) for position in (source, target)]
    chosen = jax.random.permutation(rng, parts)[partner]
    strong = (owner == chosen) | (owner == (partner + parts // 2) % parts)
    return jnp.where(strong, factor * entries, entries)


def block_levels(key, dims, cuts, low, top_value):
    def one(axis_at, shards_of):
        heights = jax.random.uniform(jax.random.fold_in(jax.random.fold_in(key, 6), axis_at), (shards_of,), jnp.float32, low / len(cuts), top_value / len(cuts))
        return jnp.repeat(jnp.exp(heights), dims[axis_at] // shards_of).reshape((-1,) + (1,) * (len(dims) - axis_at - 1))

    loudness = one(*cuts[0])
    for cut in cuts[1:]:
        loudness = loudness * one(*cut)
    return loudness


def noise(key, dims, deviation, limit, shards=(), held_as=jnp.bfloat16):
    factor_of = block_levels(key, dims, shards, -0.22, 0.18) if shards else 1.0
    array = jax.random.normal(key, dims, jnp.float32) * deviation * factor_of
    return jnp.minimum(jnp.maximum(array, -limit), limit).astype(held_as)


def bell_draw_with(stream_key, dims, scale, limit, cuts, heavy, kind=jnp.bfloat16):
    values = scale * jax.random.normal(stream_key, dims, jnp.float32)
    if cuts:
        values = values * block_levels(stream_key, dims, cuts, -0.22, 0.18)
    return jnp.clip(strengthened(values, jax.random.fold_in(stream_key, 3), *heavy), -limit, limit).astype(kind)


def setup_inputs(seed: int = 0) -> dict:
    key_of = jax.random.split(jax.random.key(seed), 10)
    return {
        "tokens": bell_draw_with(key_of[0], (TOKENS, D), 1.0, 6.0, ((0, 32),), (0, 1, 32, 2.75)),
        "cotangent": noise(key_of[1], (TOKENS, DV), TOKENS ** -0.5, 0.0390625, ((0, 32),)),
        "policy": noise(key_of[2], (D, DV), D ** -0.5, 0.09375, ((0, 32),), jnp.float32),
        "anchor": noise(key_of[3], (D, DV), D ** -0.5, 0.09375, ((0, 32),), jnp.float32),
        "moment": noise(key_of[4], (D, DV), 0.5, 3.0, ((0, 32),), jnp.float32),
        "second": jnp.clip(jnp.exp(math.log(4.0) - 2.7725887 * jax.random.uniform(key_of[5], (D, DV), jnp.float32) ** block_levels(key_of[5], (D, DV), ((0, 32),), -0.2, 0.2)), 0.25, 4.0),
        "readout": noise(key_of[6], (DV,), 1.0, 6.0, (), jnp.float32),
        "pair_index": draw_pair_index(jax.random.fold_in(key_of[9], 71), 0),
        "noisy_flags": touch_ends((jax.random.randint(key_of[8], (PAIRS,), 0, 8) < 1).astype(jnp.int32), jax.random.fold_in(key_of[8], 1), 0, 1),
    }


beta_one = 0.9
beta_two = 0.95
step_count = 20
learn_rate = 0.003
adam_epsilon = 1e-08
blend_rate = 0.6
smoothing = 0.1

def adam_update(gradient, policy, anchor, moment, second):
    moment_new = beta_one * moment + (1.0 - beta_one) * gradient
    second_new = beta_two * second + (1.0 - beta_two) * gradient * gradient
    correct_one = 1.0 - beta_one ** step_count
    correct_two = 1.0 - beta_two ** step_count
    policy_new = policy - learn_rate * (moment_new / correct_one) / (jnp.sqrt(second_new / correct_two) + adam_epsilon)
    anchor_new = blend_rate * policy_new + (1.0 - blend_rate) * anchor
    return (policy_new, anchor_new, moment_new, second_new)

def token_scores(values, readout):
    return lax.optimization_barrier(jnp.sum(jax.nn.log_sigmoid(values * readout[None, :]), axis=1))

def sequence_margin(policy_values, anchor_values, readout, sequence_length):
    token_gap = token_scores(policy_values, readout) - token_scores(anchor_values, readout)
    return lax.optimization_barrier(jnp.mean(token_gap.reshape(-1, sequence_length), axis=1))

def pair_losses(margins, pair_index, noisy_flags):
    sequence_index = jnp.arange(margins.shape[0], dtype=jnp.int32)
    chosen = lax.optimization_barrier(jnp.sum(jnp.where(pair_index[:, 0:1] == sequence_index[None, :], margins[None, :], 0.0), axis=1))
    rejected = lax.optimization_barrier(jnp.sum(jnp.where(pair_index[:, 1:2] == sequence_index[None, :], margins[None, :], 0.0), axis=1))
    margin_gap = chosen - rejected
    logit_value = jnp.where(noisy_flags == 1, -margin_gap, margin_gap)
    return -(1.0 - smoothing) * jax.nn.log_sigmoid(logit_value) - smoothing * jax.nn.log_sigmoid(-logit_value)

def reference(tokens, cotangent, policy, anchor, moment, second, readout, pair_index, noisy_flags):
    gradient = lax.dot_general(tokens, cotangent, (((0,), (0,)), ((), ())), preferred_element_type=jnp.float32)
    policy_next, anchor_next, moment_next, second_next = adam_update(gradient, policy, anchor, moment, second)
    policy_values = jnp.dot(tokens, policy_next.astype(jnp.bfloat16), preferred_element_type=jnp.float32)
    anchor_values = jnp.dot(tokens, anchor_next.astype(jnp.bfloat16), preferred_element_type=jnp.float32)
    margins = sequence_margin(policy_values, anchor_values, readout, LEN)
    pair_loss = pair_losses(margins, pair_index, noisy_flags)
    return (policy_next, anchor_next, moment_next, second_next, pair_loss)
```

```python
import functools
import jax
import jax.numpy as jnp
from jax import lax
from jax.experimental import pallas as pl
from jax.experimental.pallas import tpu as pltpu
from jax.sharding import PartitionSpec as P

LEN = 192


beta_one = 0.9
beta_two = 0.95
step_count = 20
learn_rate = 0.003
adam_epsilon = 1e-08
blend_rate = 0.6
smoothing = 0.1


def adam_update(gradient, policy, anchor, moment, second):
    moment_new = beta_one * moment + (1.0 - beta_one) * gradient
    second_new = beta_two * second + (1.0 - beta_two) * gradient * gradient
    correct_one = 1.0 - beta_one**step_count
    correct_two = 1.0 - beta_two**step_count
    policy_new = policy - learn_rate * (moment_new / correct_one) / (
        jnp.sqrt(second_new / correct_two) + adam_epsilon
    )
    anchor_new = blend_rate * policy_new + (1.0 - blend_rate) * anchor
    return (policy_new, anchor_new, moment_new, second_new)


def token_scores(values, readout):
    return jnp.sum(jax.nn.log_sigmoid(values * readout[None, :]), axis=1)


def sequence_margin(policy_values, anchor_values, readout, sequence_length):
    token_gap = token_scores(policy_values, readout) - token_scores(anchor_values, readout)
    return jnp.mean(token_gap.reshape(-1, sequence_length), axis=1)


def pair_losses(margins, pair_index, noisy_flags):
    sequence_index = jnp.arange(margins.shape[0], dtype=jnp.int32)
    chosen = jnp.sum(
        jnp.where(pair_index[:, 0:1] == sequence_index[None, :], margins[None, :], 0.0), axis=1
    )
    rejected = jnp.sum(
        jnp.where(pair_index[:, 1:2] == sequence_index[None, :], margins[None, :], 0.0), axis=1
    )
    margin_gap = chosen - rejected
    logit_value = jnp.where(noisy_flags == 1, -margin_gap, margin_gap)
    return -(1.0 - smoothing) * jax.nn.log_sigmoid(logit_value) - smoothing * jax.nn.log_sigmoid(
        -logit_value
    )


def shards(tokens, cotangent, policy, anchor, moment, second, readout, pair_index, noisy_flags):
    part_sum = lax.psum_scatter(
        lax.dot_general(
            tokens, cotangent, (((0,), (0,)), ((), ())), preferred_element_type=jnp.float32
        ),
        "fsdp",
        scatter_dimension=0,
        tiled=True,
    )
    gradient = lax.psum(part_sum.astype(jnp.bfloat16), "rep").astype(jnp.float32)
    policy_next, anchor_next, moment_next, second_next = adam_update(
        gradient, policy, anchor, moment, second
    )
    policy_half = policy_next.astype(jnp.bfloat16)
    anchor_half = anchor_next.astype(jnp.bfloat16)
    policy_whole = lax.all_gather(policy_half, "fsdp", axis=0, tiled=True)
    anchor_whole = lax.all_gather(anchor_half, "fsdp", axis=0, tiled=True)
    policy_values = jnp.dot(tokens, policy_whole, preferred_element_type=jnp.float32)
    anchor_values = jnp.dot(tokens, anchor_whole, preferred_element_type=jnp.float32)
    margins_own = sequence_margin(policy_values, anchor_values, readout, LEN)
    all_margins = lax.all_gather(margins_own, ("rep", "fsdp"), axis=0, tiled=True)
    pair_loss = pair_losses(all_margins, pair_index, noisy_flags)
    return (policy_next, anchor_next, moment_next, second_next, pair_loss)


STEP_ORDER = (2, 1, 3, 0)
MESH_ID = pl.DeviceIdType.MESH


def fused_kernel(
    sizes,
    tokens,
    cotangent,
    policy,
    anchor,
    moment,
    second,
    readout,
    policy_out,
    anchor_out,
    moment_out,
    second_out,
    margin_out,
    tok,
    cot,
    cot_t,
    par,
    send_a1,
    recv_a1,
    keep_a,
    send_b1,
    recv_b1,
    keep_b,
    send_a2,
    recv_a2,
    send_b2,
    recv_b2,
    send_z,
    recv_z,
    grad_own,
    result,
    weights,
    acc,
    score_own,
    score_pair,
    table,
    local_sem,
    swap_send,
    swap_recv,
    rs_send,
    rs_recv,
    out_send,
    out_recv,
    z_send,
    z_recv,
    g2_send,
    g2_recv,
    g3_send,
    g3_recv,
    m_send,
    m_recv,
):
    n, rows, tokens_own, half, depth, seq_own = sizes
    block = 2 * rows
    span = 4 * block
    low = half // 2
    me = lax.axis_index("fsdp")
    core = me % 2
    px = (me // 2) % 2
    py = (me // 4) % 2
    pz = me // 8
    chip = me // 2
    mate = me + 1 - 2 * core
    x_mate = me + 2 - 4 * px
    y_mate = me + 4 - 8 * py

    def z_mate(shift):
        return (me + 8 * shift) % n

    def remote(src, dst, send_sem, recv_sem, device):
        return pltpu.make_async_remote_copy(
            src_ref=src,
            dst_ref=dst,
            send_sem=send_sem,
            recv_sem=recv_sem,
            device_id={"fsdp": device},
            device_id_type=MESH_ID,
        )

    barrier = pltpu.get_barrier_semaphore()
    others = [mate, x_mate, y_mate] + [z_mate(s) for s in (1, 2, 3)]
    for other in others:
        pl.semaphore_signal(barrier, inc=1, device_id={"fsdp": other}, device_id_type=MESH_ID)

    mine = pl.ds(pl.multiple_of(core * half, half), half)
    theirs = pl.ds(pl.multiple_of((1 - core) * half, half), half)
    params = (policy, anchor, moment, second)

    def columns(s):
        z_to = (pz + s) % 4
        return pl.ds(pl.multiple_of(z_to * span, span), span)

    cot_local = pltpu.make_async_copy(cotangent.at[:, mine], cot.at[core], local_sem.at[4])
    cot_local.start()
    tok_local = {}
    for s in STEP_ORDER:
        tok_local[s] = pltpu.make_async_copy(
            tokens.at[:, columns(s)], tok.at[core, :, columns(s)], local_sem.at[s]
        )
        tok_local[s].start()
    par_local = []
    for a in range(4):
        copy = pltpu.make_async_copy(params[a].at[:, mine], par.at[a, core], local_sem.at[5 + a])
        copy.start()
        par_local.append(copy)

    pl.semaphore_wait(barrier, len(others))

    sends = []
    cot_swap = remote(cotangent.at[:, theirs], cot.at[core], swap_send.at[4], swap_recv.at[4], mate)
    cot_swap.start()
    sends.append(cot_swap)
    tok_swap = {}
    for s in STEP_ORDER:
        tok_swap[s] = remote(
            tokens.at[:, columns(s)],
            tok.at[core, :, columns(s)],
            swap_send.at[s],
            swap_recv.at[s],
            mate,
        )
        tok_swap[s].start()
        sends.append(tok_swap[s])
    par_swap = []
    for a in range(4):
        copy = remote(
            params[a].at[:, theirs], par.at[a, core], swap_send.at[5 + a], swap_recv.at[5 + a], mate
        )
        copy.start()
        par_swap.append(copy)
        sends.append(copy)

    cot_local.wait()
    cot_swap.wait_recv()
    for r in range(2):
        cot_t[:, r * tokens_own : (r + 1) * tokens_own] = (
            cot[r].astype(jnp.float32).T.astype(jnp.bfloat16)
        )

    def first(s):
        tok_local[s].wait()
        tok_swap[s].wait_recv()

    def block_gradient(s, dy, dx):
        target = ((pz + s) % 4) * 4 + ((py + dy) % 2) * 2 + (px + dx) % 2
        where = pl.ds(pl.multiple_of(target * block, block), block)
        total = jnp.dot(
            cot_t[:, :tokens_own], tok[0, :, where], preferred_element_type=jnp.float32
        )
        total += jnp.dot(
            cot_t[:, tokens_own:], tok[1, :, where], preferred_element_type=jnp.float32
        )
        if dx == 1:
            send_a1[s, dy] = total[:low].astype(jnp.bfloat16)
        else:
            keep_a[s, dy] = total[:low]
        if dy == 1:
            send_b1[s, dx] = total[low:].astype(jnp.bfloat16)
        else:
            keep_b[s, dx] = total[low:]

    hops = {}

    def hop(name, s, slot, src, dst, device):
        copy = remote(src, dst, rs_send.at[slot, s], rs_recv.at[slot, s], device)
        copy.start()
        hops[name, s] = copy
        sends.append(copy)

    def stage_one(s):
        first(s)
        block_gradient(s, 1, 1)
        block_gradient(s, 0, 1)
        hop("a1", s, 0, send_a1.at[s], recv_a1.at[s], x_mate)
        block_gradient(s, 1, 0)
        hop("b1", s, 1, send_b1.at[s], recv_b1.at[s], y_mate)
        block_gradient(s, 0, 0)

    def stage_two(s):
        hops["a1", s].wait_recv()
        send_a2[s] = (keep_a[s, 1] + recv_a1[s, 1].astype(jnp.float32)).astype(jnp.bfloat16)
        hop("a2", s, 2, send_a2.at[s], recv_a2.at[s], y_mate)
        hops["b1", s].wait_recv()
        send_b2[s] = (keep_b[s, 1] + recv_b1[s, 1].astype(jnp.float32)).astype(jnp.bfloat16)
        hop("b2", s, 3, send_b2.at[s], recv_b2.at[s], x_mate)

    def stage_three(s):
        hops["a2", s].wait_recv()
        total_a = keep_a[s, 0] + recv_a1[s, 0].astype(jnp.float32) + recv_a2[s].astype(jnp.float32)
        hops["b2", s].wait_recv()
        total_b = keep_b[s, 0] + recv_b1[s, 0].astype(jnp.float32) + recv_b2[s].astype(jnp.float32)
        if s == 0:
            grad_own[:low] = total_a
            grad_own[low:] = total_b
        else:
            send_z[s - 1, :low] = total_a.astype(jnp.bfloat16)
            send_z[s - 1, low:] = total_b.astype(jnp.bfloat16)
            hop("z", s, 4, send_z.at[s - 1], recv_z.at[s - 1], z_mate(s))

    for i in range(len(STEP_ORDER) + 2):
        if i < len(STEP_ORDER):
            stage_one(STEP_ORDER[i])
        if 1 <= i <= len(STEP_ORDER):
            stage_two(STEP_ORDER[i - 1])
        if i >= 2:
            stage_three(STEP_ORDER[i - 2])

    for a in range(4):
        par_local[a].wait()
        par_swap[a].wait_recv()
    for s in STEP_ORDER[:3]:
        hops["z", s].wait_recv()
    gradient = grad_own[...]
    for s in range(3):
        gradient += recv_z[s].astype(jnp.float32)
    gradient = gradient.T
    home = chip * block
    for r in range(2):
        updated = adam_update(
            gradient[r * rows : (r + 1) * rows], par[0, r], par[1, r], par[2, r], par[3, r]
        )
        for a in range(4):
            result[a, r] = updated[a]
        for m in range(2):
            weights[m, pl.ds(pl.multiple_of(home + r * rows, rows), rows), :] = updated[m].astype(
                jnp.bfloat16
            )

    top = pz // 2
    near = pz + top * (3 - 2 * pz)

    def source(t):
        there = (near, 1 - near, 2, 3)[t]
        return there + top * (3 - 2 * there)

    def part(m, k):
        return weights.at[m, pl.ds(pl.multiple_of(k * block, block), block), :]

    def z_copy(m, zz, way):
        ref = part(m, zz * 4 + py * 2 + px)
        device = z_mate(1) if way == 0 else z_mate(3)
        return remote(ref, ref, z_send.at[way, m, zz], z_recv.at[m, zz], device)

    def z_forward(zz, act):
        @pl.when(jnp.logical_and(zz <= pz, pz < 3))
        def _():
            for m in range(2):
                act(z_copy(m, zz, 0))

        @pl.when(jnp.logical_and(zz >= pz, pz > 0))
        def _():
            for m in range(2):
                act(z_copy(m, zz, 1))

    gathers = {}

    def gather_two(t, zz):
        for m in range(2):
            ref = part(m, zz * 4 + py * 2 + px)
            device = y_mate if m == 0 else x_mate
            copy = remote(ref, ref, g2_send.at[t, m], g2_recv.at[t, m], device)
            copy.start()
            gathers[2, t, m] = copy
            sends.append(copy)

    def gather_three(t, zz, late, m):
        ky = (py + late) % 2 if m == 0 else py
        kx = px if m == 0 else (px + late) % 2
        ref = part(m, zz * 4 + ky * 2 + kx)
        device = x_mate if m == 0 else y_mate
        copy = remote(ref, ref, g3_send.at[t, late, m], g3_recv.at[t, late, m], device)
        copy.start()
        gathers[3, t, late, m] = copy
        sends.append(copy)

    tile = tokens_own // 2
    scale = readout[core]

    def score_sum(values):
        low_part = jnp.minimum(values, 0.0).reshape(LEN // 8, 8, half)
        factor = (1.0 + jnp.exp(-jnp.abs(values))).reshape(LEN // 8, 8, half)
        product = factor[0]
        for j in range(1, LEN // 8):
            product = product * factor[j]
        return jnp.sum(low_part, axis=0) - jnp.log(product)

    def compute(t, zz):
        for late in range(2):
            for m in range(2):
                gathers[3, t, late, m].wait_recv()
        where = pl.ds(pl.multiple_of(zz * span, span), span)

        @pl.loop(0, 4)
        def _(i):
            r = i // 2
            at = pl.ds(pl.multiple_of((i % 2) * tile, tile), tile)
            lhs = tok[r, at, where]
            values = []
            for m in range(2):
                value = jnp.dot(lhs, weights[m, where, :], preferred_element_type=jnp.float32)
                if t > 0:
                    value = value + acc[m, i]
                if t < 3:
                    acc[m, i] = value
                else:
                    acc[m, i] = value * scale
            if t == 3:
                for j in range(tile // LEN):
                    gap = score_sum(acc[0, i, j * LEN : (j + 1) * LEN]) - score_sum(
                        acc[1, i, j * LEN : (j + 1) * LEN]
                    )
                    gap = jnp.sum(gap, axis=0, keepdims=True)
                    gap = jnp.sum(gap, axis=1, keepdims=True)
                    score_own[pl.ds(i * (tile // LEN) + j, 1), :] = jnp.broadcast_to(gap, (1, 128))

    waits = []
    for t in range(4):
        zz = source(t)
        if t > 0:
            for m in range(2):
                z_copy(m, zz, 0).wait_recv()
        z_forward(zz, lambda copy: copy.start())
        gather_two(t, zz)
        gather_three(t, zz, 0, 0)
        gather_three(t, zz, 0, 1)
        if t == 0:
            outs = (policy_out, anchor_out, moment_out, second_out)
            for a in range(4):
                copy = pltpu.make_async_copy(
                    result.at[a, core], outs[a].at[:, mine], local_sem.at[9 + a]
                )
                copy.start()
                waits.append(copy)
                copy = remote(
                    result.at[a, 1 - core],
                    outs[a].at[:, mine],
                    out_send.at[a],
                    out_recv.at[a],
                    mate,
                )
                copy.start()
                waits.append(copy)
        for m in range(2):
            gathers[2, t, m].wait_recv()
            gather_three(t, zz, 1, m)
        if t > 0:
            compute(t - 1, source(t - 1))
    compute(3, source(3))

    copy = remote(score_own, score_pair, m_send.at[0], m_recv.at[0], mate)
    copy.start()
    sends.append(copy)
    copy.wait_recv()
    table[chip] = (score_own[...] + score_pair[...]) * (1.0 / LEN)

    def table_copy(start, count, slot, device):
        ref = table.at[pl.ds(start, count)]
        copy = remote(ref, ref, m_send.at[slot], m_recv.at[slot], device)
        copy.start()
        sends.append(copy)
        return copy

    table_copy(chip, 1, 1, x_mate).wait_recv()
    table_copy(chip - px, 2, 2, y_mate).wait_recv()
    last = [table_copy(pz * 4, 4, 2 + s, z_mate(s)) for s in (1, 2, 3)]
    for copy in last:
        copy.wait_recv()
    for copy in waits:
        copy.wait()
    for copy in sends:
        copy.wait_send()
    for t in range(4):
        z_forward(source(t), lambda copy: copy.wait_send())
    margin_out[...] = table[...]


def fused_shards(n, tokens, cotangent, policy, anchor, moment, second, readout, pair_index, noisy_flags):
    tokens_own, depth = tokens.shape
    rows, channels = policy.shape
    half = channels // 2
    block = 2 * rows
    low = half // 2
    seq_chip = 2 * tokens_own // LEN
    sizes = (n, rows, tokens_own, half, depth, seq_chip // 2)
    bf, f32 = jnp.bfloat16, jnp.float32
    vmem, dma = pltpu.VMEM, pltpu.SemaphoreType.DMA
    hbm = pl.BlockSpec(memory_space=pl.ANY)
    whole = pl.BlockSpec(memory_space=pltpu.VMEM)
    weight = jax.ShapeDtypeStruct((rows, channels), f32)
    policy_next, anchor_next, moment_next, second_next, table = pl.pallas_call(
        functools.partial(fused_kernel, sizes),
        out_shape=(weight,) * 4 + (jax.ShapeDtypeStruct((n // 2, seq_chip, 128), f32),),
        in_specs=[hbm] * 6 + [whole],
        out_specs=(hbm,) * 4 + (whole,),
        scratch_shapes=[
            vmem((2, tokens_own, depth), bf),
            vmem((2, tokens_own, half), bf),
            vmem((half, 2 * tokens_own), bf),
            vmem((4, 2, rows, half), f32),
            vmem((4, 2, low, block), bf),
            vmem((4, 2, low, block), bf),
            vmem((4, 2, low, block), f32),
            vmem((4, 2, low, block), bf),
            vmem((4, 2, low, block), bf),
            vmem((4, 2, low, block), f32),
            vmem((4, low, block), bf),
            vmem((4, low, block), bf),
            vmem((4, low, block), bf),
            vmem((4, low, block), bf),
            vmem((3, half, block), bf),
            vmem((3, half, block), bf),
            vmem((half, block), f32),
            vmem((4, 2, rows, half), f32),
            vmem((2, depth, half), bf),
            vmem((2, 4, tokens_own // 2, half), f32),
            vmem((seq_chip, 128), f32),
            vmem((seq_chip, 128), f32),
            vmem((n // 2, seq_chip, 128), f32),
            dma((13,)),
            dma((9,)),
            dma((9,)),
            dma((5, 4)),
            dma((5, 4)),
            dma((4,)),
            dma((4,)),
            dma((2, 2, 4)),
            dma((2, 4)),
            dma((4, 2)),
            dma((4, 2)),
            dma((4, 2, 2)),
            dma((4, 2, 2)),
            dma((6,)),
            dma((6,)),
        ],
        compiler_params=pltpu.CompilerParams(
            collective_id=0, has_side_effects=True, vmem_limit_bytes=56 * 1024 * 1024
        ),
    )(
        tokens,
        cotangent,
        policy,
        anchor,
        moment,
        second,
        readout.reshape(2, 1, half),
    )
    margins = table[:, :, 0].reshape(-1)
    pair_loss = pair_losses(margins, pair_index, noisy_flags)
    return (policy_next, anchor_next, moment_next, second_next, pair_loss)


def solution(mesh):
    placed = (
        P(("rep", "fsdp"), None),
        P(("rep", "fsdp"), None),
        P("fsdp", None),
        P("fsdp", None),
        P("fsdp", None),
        P("fsdp", None),
        P(),
        P(("rep", "fsdp"), None),
        P(("rep", "fsdp")),
    )
    n = mesh.shape["fsdp"]
    body = shards
    if mesh.shape["rep"] == 1 and n // 8 == len(STEP_ORDER):
        body = functools.partial(fused_shards, n)
    return jax.shard_map(
        body,
        mesh=mesh,
        in_specs=placed,
        out_specs=(
            P("fsdp", None),
            P("fsdp", None),
            P("fsdp", None),
            P("fsdp", None),
            P(("rep", "fsdp")),
        ),
        check_vma=False,
    )
```

```python
import functools
import itertools
import jax
import jax.numpy as jnp
from jax import lax
from jax.experimental import pallas as pl
from jax.experimental.pallas import tpu as pltpu
from jax.sharding import PartitionSpec as P

LEN = 192


beta_one = 0.9
beta_two = 0.95
step_count = 20
learn_rate = 0.003
adam_epsilon = 1e-08
blend_rate = 0.6
smoothing = 0.1


def adam_update(gradient, policy, anchor, moment, second):
    moment_new = beta_one * moment + (1.0 - beta_one) * gradient
    second_new = beta_two * second + (1.0 - beta_two) * gradient * gradient
    correct_one = 1.0 - beta_one**step_count
    correct_two = 1.0 - beta_two**step_count
    policy_new = policy - learn_rate * (moment_new / correct_one) / (
        jnp.sqrt(second_new / correct_two) + adam_epsilon
    )
    anchor_new = blend_rate * policy_new + (1.0 - blend_rate) * anchor
    return (policy_new, anchor_new, moment_new, second_new)


def token_scores(values, readout):
    return jnp.sum(jax.nn.log_sigmoid(values * readout[None, :]), axis=1)


def sequence_margin(policy_values, anchor_values, readout, sequence_length):
    token_gap = token_scores(policy_values, readout) - token_scores(anchor_values, readout)
    return jnp.mean(token_gap.reshape(-1, sequence_length), axis=1)


def pair_losses(margins, pair_index, noisy_flags):
    sequence_index = jnp.arange(margins.shape[0], dtype=jnp.int32)
    chosen = jnp.sum(
        jnp.where(pair_index[:, 0:1] == sequence_index[None, :], margins[None, :], 0.0), axis=1
    )
    rejected = jnp.sum(
        jnp.where(pair_index[:, 1:2] == sequence_index[None, :], margins[None, :], 0.0), axis=1
    )
    margin_gap = chosen - rejected
    logit_value = jnp.where(noisy_flags == 1, -margin_gap, margin_gap)
    return -(1.0 - smoothing) * jax.nn.log_sigmoid(logit_value) - smoothing * jax.nn.log_sigmoid(
        -logit_value
    )


def shards(tokens, cotangent, policy, anchor, moment, second, readout, pair_index, noisy_flags):
    part_sum = lax.psum_scatter(
        lax.dot_general(
            tokens, cotangent, (((0,), (0,)), ((), ())), preferred_element_type=jnp.float32
        ),
        "fsdp",
        scatter_dimension=0,
        tiled=True,
    )
    gradient = lax.psum(part_sum.astype(jnp.bfloat16), "rep").astype(jnp.float32)
    policy_next, anchor_next, moment_next, second_next = adam_update(
        gradient, policy, anchor, moment, second
    )
    policy_half = policy_next.astype(jnp.bfloat16)
    anchor_half = anchor_next.astype(jnp.bfloat16)
    policy_whole = lax.all_gather(policy_half, "fsdp", axis=0, tiled=True)
    anchor_whole = lax.all_gather(anchor_half, "fsdp", axis=0, tiled=True)
    policy_values = jnp.dot(tokens, policy_whole, preferred_element_type=jnp.float32)
    anchor_values = jnp.dot(tokens, anchor_whole, preferred_element_type=jnp.float32)
    margins_own = sequence_margin(policy_values, anchor_values, readout, LEN)
    all_margins = lax.all_gather(margins_own, ("rep", "fsdp"), axis=0, tiled=True)
    pair_loss = pair_losses(all_margins, pair_index, noisy_flags)
    return (policy_next, anchor_next, moment_next, second_next, pair_loss)


STEP_ORDER = (2, 1, 3, 0)
MESH_ID = pl.DeviceIdType.MESH


def fused_kernel(
    sizes,
    tokens,
    cotangent,
    policy,
    anchor,
    moment,
    second,
    readout,
    gradient_out,
    margin_out,
    tok,
    cot,
    cot_t,
    par,
    send_a1,
    recv_a1,
    keep_a,
    send_b1,
    recv_b1,
    keep_b,
    send_a2,
    recv_a2,
    send_b2,
    recv_b2,
    send_z,
    recv_z,
    grad_own,
    result,
    weights,
    acc,
    table,
    local_sem,
    swap_send,
    swap_recv,
    rs_send,
    rs_recv,
    out_send,
    out_recv,
    z_send,
    z_recv,
    far_send,
    far_recv,
    g2_send,
    g2_recv,
    g3_send,
    g3_recv,
    m_send,
    m_recv,
):
    n, rows, tokens_own, half, depth, seq_own = sizes
    block = 2 * rows
    span = 4 * block
    low = half // 2
    me = lax.axis_index("fsdp")
    core = me % 2
    px = (me // 2) % 2
    py = (me // 4) % 2
    pz = me // 8
    chip = me // 2
    mate = me + 1 - 2 * core
    x_mate = me + 2 - 4 * px
    y_mate = me + 4 - 8 * py

    def z_mate(shift):
        return (me + 8 * shift) % n

    def remote(src, dst, send_sem, recv_sem, device):
        return pltpu.make_async_remote_copy(
            src_ref=src,
            dst_ref=dst,
            send_sem=send_sem,
            recv_sem=recv_sem,
            device_id={"fsdp": device},
            device_id_type=MESH_ID,
        )

    barrier = pltpu.get_barrier_semaphore()
    plane = [
        me + dc * (1 - 2 * core) + dx * (2 - 4 * px) + dy * (4 - 8 * py)
        for dc, dx, dy in itertools.product((0, 1), repeat=3)
    ][1:]
    others = plane + [z_mate(s) for s in (1, 2, 3)]
    for other in others:
        pl.semaphore_signal(barrier, inc=1, device_id={"fsdp": other}, device_id_type=MESH_ID)

    mine = pl.ds(pl.multiple_of(core * half, half), half)
    theirs = pl.ds(pl.multiple_of((1 - core) * half, half), half)
    params = (policy, anchor, moment, second)

    pair = 2 * block

    def columns(s, dy):
        start = ((pz + s) % 4) * span + ((py + dy) % 2) * pair
        return pl.ds(pl.multiple_of(start, pair), pair)

    pieces = [(s, dy) for s in STEP_ORDER for dy in (1, 0)]

    cot_local = pltpu.make_async_copy(cotangent.at[:, mine], cot.at[core], local_sem.at[4])
    cot_local.start()
    tok_local = {}
    for i, (s, dy) in enumerate(pieces):
        tok_local[s, dy] = pltpu.make_async_copy(
            tokens.at[:, columns(s, dy)], tok.at[core, :, columns(s, dy)], local_sem.at[10 + i]
        )
        tok_local[s, dy].start()
    par_local = []
    for a in range(4):
        copy = pltpu.make_async_copy(params[a].at[:, mine], par.at[a, core], local_sem.at[5 + a])
        copy.start()
        par_local.append(copy)

    pl.semaphore_wait(barrier, len(others))

    sends = []
    cot_swap = remote(cotangent.at[:, theirs], cot.at[core], swap_send.at[4], swap_recv.at[4], mate)
    cot_swap.start()
    sends.append(cot_swap)
    tok_swap = {}
    for i, (s, dy) in enumerate(pieces):
        tok_swap[s, dy] = remote(
            tokens.at[:, columns(s, dy)],
            tok.at[core, :, columns(s, dy)],
            swap_send.at[10 + i],
            swap_recv.at[10 + i],
            mate,
        )
        tok_swap[s, dy].start()
        sends.append(tok_swap[s, dy])
    par_swap = []
    for a in range(4):
        copy = remote(
            params[a].at[:, theirs], par.at[a, core], swap_send.at[5 + a], swap_recv.at[5 + a], mate
        )
        copy.start()
        par_swap.append(copy)
        sends.append(copy)

    cot_local.wait()
    cot_swap.wait_recv()
    for r in range(2):
        cot_t[:, r * tokens_own : (r + 1) * tokens_own] = (
            cot[r].astype(jnp.float32).T.astype(jnp.bfloat16)
        )

    def first(s, dy):
        tok_local[s, dy].wait()
        tok_swap[s, dy].wait_recv()

    def block_gradient(s, dy, dx):
        target = ((pz + s) % 4) * 4 + ((py + dy) % 2) * 2 + (px + dx) % 2
        where = pl.ds(pl.multiple_of(target * block, block), block)
        total = jnp.dot(
            cot_t[:, :tokens_own], tok[0, :, where], preferred_element_type=jnp.float32
        )
        total += jnp.dot(
            cot_t[:, tokens_own:], tok[1, :, where], preferred_element_type=jnp.float32
        )
        if dx == 1:
            send_a1[s, dy] = total[:low].astype(jnp.bfloat16)
        else:
            keep_a[s, dy] = total[:low]
        if dy == 1:
            send_b1[s, dx] = total[low:].astype(jnp.bfloat16)
        else:
            keep_b[s, dx] = total[low:]

    hops = {}

    def hop(name, s, slot, src, dst, device):
        copy = remote(src, dst, rs_send.at[slot, s], rs_recv.at[slot, s], device)
        copy.start()
        hops[name, s] = copy
        sends.append(copy)

    def stage_one(s):
        first(s, 1)
        block_gradient(s, 1, 1)
        block_gradient(s, 1, 0)
        hop("b1", s, 1, send_b1.at[s], recv_b1.at[s], y_mate)
        first(s, 0)
        block_gradient(s, 0, 1)
        hop("a1", s, 0, send_a1.at[s], recv_a1.at[s], x_mate)
        block_gradient(s, 0, 0)

    def stage_two(s):
        hops["a1", s].wait_recv()
        send_a2[s] = (keep_a[s, 1] + recv_a1[s, 1].astype(jnp.float32)).astype(jnp.bfloat16)
        hop("a2", s, 2, send_a2.at[s], recv_a2.at[s], y_mate)
        hops["b1", s].wait_recv()
        send_b2[s] = (keep_b[s, 1] + recv_b1[s, 1].astype(jnp.float32)).astype(jnp.bfloat16)
        hop("b2", s, 3, send_b2.at[s], recv_b2.at[s], x_mate)

    def stage_three(s):
        hops["a2", s].wait_recv()
        total_a = keep_a[s, 0] + recv_a1[s, 0].astype(jnp.float32) + recv_a2[s].astype(jnp.float32)
        hops["b2", s].wait_recv()
        total_b = keep_b[s, 0] + recv_b1[s, 0].astype(jnp.float32) + recv_b2[s].astype(jnp.float32)
        if s == 0:
            grad_own[:low] = total_a
            grad_own[low:] = total_b
        else:
            send_z[s - 1, :low] = total_a.astype(jnp.bfloat16)
            send_z[s - 1, low:] = total_b.astype(jnp.bfloat16)
            hop("z", s, 4, send_z.at[s - 1], recv_z.at[s - 1], z_mate(s))

    for i in range(len(STEP_ORDER) + 2):
        if i < len(STEP_ORDER):
            stage_one(STEP_ORDER[i])
        if 1 <= i <= len(STEP_ORDER):
            stage_two(STEP_ORDER[i - 1])
        if i >= 2:
            stage_three(STEP_ORDER[i - 2])

    for a in range(4):
        par_local[a].wait()
        par_swap[a].wait_recv()
    for s in STEP_ORDER[:3]:
        hops["z", s].wait_recv()
    gradient = grad_own[...]
    for s in range(3):
        gradient += recv_z[s].astype(jnp.float32)
    gradient = gradient.T
    home = chip * block
    for r in range(2):
        updated = adam_update(
            gradient[r * rows : (r + 1) * rows], par[0, r], par[1, r], par[2, r], par[3, r]
        )
        result[r] = gradient[r * rows : (r + 1) * rows]
        for m in range(2):
            weights[m, pl.ds(pl.multiple_of(home + r * rows, rows), rows), :] = updated[m].astype(
                jnp.bfloat16
            )

    top = pz // 2
    near = pz + top * (3 - 2 * pz)

    def source(t):
        there = (near, 1 - near, 2, 3)[t]
        return there + top * (3 - 2 * there)

    def part(m, k):
        return weights.at[m, pl.ds(pl.multiple_of(k * block, block), block), :]

    def z_copy(m, zz, way):
        ref = part(m, zz * 4 + py * 2 + px)
        device = z_mate(1) if way == 0 else z_mate(3)
        return remote(ref, ref, z_send.at[way, m, zz], z_recv.at[m, zz], device)

    def z_forward(zz, act):
        @pl.when(jnp.logical_and(zz <= pz, pz < 3))
        def _():
            for m in range(2):
                act(z_copy(m, zz, 0))

        @pl.when(jnp.logical_and(zz >= pz, pz > 0))
        def _():
            for m in range(2):
                act(z_copy(m, zz, 1))

    gathers = {}

    def gather_two(t, zz):
        for m in range(2):
            ref = part(m, zz * 4 + py * 2 + px)
            device = y_mate if m == 0 else x_mate
            copy = remote(ref, ref, g2_send.at[t, m], g2_recv.at[t, m], device)
            copy.start()
            gathers[2, t, m] = copy
            sends.append(copy)

    across = 3 - 2 * py - px

    def piece(k, second_half):
        return pl.ds(pl.multiple_of(k * block + second_half * rows, rows), rows)

    def far_copy(m, zz, s, device):
        ref = weights.at[m, piece(zz * 4 + across, 1), :]
        return remote(ref, ref, far_send.at[m, s - 1], far_recv.at[m, zz], device)

    def far_start():
        for s in (2, 1, 3):
            for m in range(2):
                copy = far_copy(m, pz, s, z_mate(s))
                copy.start()
                sends.append(copy)

    def gather_three(t, zz, late, m):
        ky = (py + late) % 2 if m == 0 else py
        kx = px if m == 0 else (px + late) % 2
        ref = part(m, zz * 4 + ky * 2 + kx)
        if late == 1 and t > 0:
            ref = weights.at[m, piece(zz * 4 + ky * 2 + kx, 0), :]
        device = x_mate if m == 0 else y_mate
        copy = remote(ref, ref, g3_send.at[t, late, m], g3_recv.at[t, late, m], device)
        copy.start()
        gathers[3, t, late, m] = copy
        sends.append(copy)

    tile = tokens_own // 2
    scale = readout[core]

    def score_sum(values):
        low_part = jnp.minimum(values, 0.0).reshape(LEN // 8, 8, half)
        factor = (1.0 + jnp.exp(-jnp.abs(values))).reshape(LEN // 8, 8, half)
        product = factor[0]
        for j in range(1, LEN // 8):
            product = product * factor[j]
        return jnp.sum(low_part, axis=0) - jnp.log(product)

    def arrived(t, zz, late):
        for m in range(2):
            gathers[3, t, late, m].wait_recv()
            if late == 1 and t > 0:
                far_copy(m, zz, 1, z_mate(1)).wait_recv()

    def compute(t, zz):
        where = pl.ds(pl.multiple_of(zz * span, span), span)

        @pl.loop(0, 4)
        def _(i):
            at = pl.ds(pl.multiple_of((i % 2) * tile, tile), tile)
            lhs = tok[i // 2, at, where]
            for m in range(2):
                value = jnp.dot(lhs, weights[m, where, :], preferred_element_type=jnp.float32)
                acc[m, i] = value if t == 0 else acc[m, i] + value

    def spot(zz, dy, dx):
        k = zz * 4 + ((py + dy) % 2) * 2 + (px + dx) % 2
        return pl.ds(pl.multiple_of(k * block, block), block)

    def compute_near(zz):
        @pl.loop(0, 4)
        def _(i):
            at = pl.ds(pl.multiple_of((i % 2) * tile, tile), tile)
            for m in range(2):
                value = acc[m, i]
                for dy, dx in ((0, 0), (0, 1), (1, 0)):
                    where = spot(zz, dy, dx)
                    value += jnp.dot(
                        tok[i // 2, at, where],
                        weights[m, where, :],
                        preferred_element_type=jnp.float32,
                    )
                acc[m, i] = value

    def compute_last(zz):
        where = spot(zz, 1, 1)

        @pl.loop(0, 4)
        def _(i):
            at = pl.ds(pl.multiple_of((i % 2) * tile, tile), tile)
            lhs = tok[i // 2, at, where]
            for m in range(2):
                value = jnp.dot(lhs, weights[m, where, :], preferred_element_type=jnp.float32)
                acc[m, i] = (value + acc[m, i]) * scale
            for j in range(tile // LEN):
                gap = score_sum(acc[0, i, j * LEN : (j + 1) * LEN]) - score_sum(
                    acc[1, i, j * LEN : (j + 1) * LEN]
                )
                gap = jnp.sum(gap, axis=0, keepdims=True)
                gap = jnp.sum(gap, axis=1, keepdims=True)
                table[core, chip, pl.ds(i * (tile // LEN) + j, 1), :] = jnp.broadcast_to(
                    gap * (1.0 / LEN), (1, 128)
                )

    waits = []
    for t in range(4):
        zz = source(t)
        if t > 0:
            for m in range(2):
                z_copy(m, zz, 0).wait_recv()
        z_forward(zz, lambda copy: copy.start())
        gather_two(t, zz)
        gather_three(t, zz, 0, 0)
        gather_three(t, zz, 0, 1)
        if t == 0:
            copy = pltpu.make_async_copy(result.at[core], gradient_out.at[:, mine], local_sem.at[9])
            copy.start()
            waits.append(copy)
            copy = remote(
                result.at[1 - core], gradient_out.at[:, mine], out_send.at[0], out_recv.at[0], mate
            )
            copy.start()
            waits.append(copy)
        for m in range(2):
            gathers[2, t, m].wait_recv()
            gather_three(t, zz, 1, m)
        if t > 0:
            arrived(t - 1, source(t - 1), 0)
            arrived(t - 1, source(t - 1), 1)
            if t == 1:
                far_start()
            compute(t - 1, source(t - 1))
    arrived(3, source(3), 0)
    compute_near(source(3))
    arrived(3, source(3), 1)
    compute_last(source(3))

    def table_copy(ref, slot, device):
        copy = remote(ref, ref, m_send.at[slot], m_recv.at[slot], device)
        copy.start()
        sends.append(copy)
        return copy

    near_copies = [
        table_copy(table.at[core, pl.ds(chip, 1)], i, device) for i, device in enumerate(plane)
    ]
    for copy in near_copies:
        copy.wait_recv()
    last = [
        table_copy(table.at[:, pl.ds(pz * 4, 4)], 6 + s, z_mate(s)) for s in (2, 1, 3)
    ]
    for copy in last:
        copy.wait_recv()
    for copy in waits:
        copy.wait()
    for copy in sends:
        copy.wait_send()
    for t in range(4):
        z_forward(source(t), lambda copy: copy.wait_send())
    margin_out[...] = table[...]


def finish_kernel(
    gradient,
    policy,
    anchor,
    moment,
    second,
    table,
    pair_index,
    noisy_flags,
    policy_out,
    anchor_out,
    moment_out,
    second_out,
    loss_out,
):
    updated = adam_update(gradient[...], policy[...], anchor[...], moment[...], second[...])
    for out, value in zip((policy_out, anchor_out, moment_out, second_out), updated):
        out[...] = value
    margins = table[0] + table[1]
    sequence = lax.broadcasted_iota(jnp.int32, margins.shape, 0)

    def margin_of(index):
        return jnp.sum(jnp.where(sequence == index, margins, 0.0), axis=0, keepdims=True)

    for p in range(noisy_flags.shape[0]):
        gap = margin_of(pair_index[p, 0]) - margin_of(pair_index[p, 1])
        gap = jnp.where(noisy_flags[p] == 1, -gap, gap)
        tail = jnp.log(1.0 + jnp.exp(-jnp.abs(gap)))
        loss = (1.0 - smoothing) * (tail - jnp.minimum(gap, 0.0)) + smoothing * (
            tail + jnp.maximum(gap, 0.0)
        )
        loss_out[p] = loss[0, 0]


def fused_shards(n, tokens, cotangent, policy, anchor, moment, second, readout, pair_index, noisy_flags):
    tokens_own, depth = tokens.shape
    rows, channels = policy.shape
    half = channels // 2
    block = 2 * rows
    low = half // 2
    seq_chip = 2 * tokens_own // LEN
    sizes = (n, rows, tokens_own, half, depth, seq_chip // 2)
    bf, f32 = jnp.bfloat16, jnp.float32
    vmem, dma = pltpu.VMEM, pltpu.SemaphoreType.DMA
    hbm = pl.BlockSpec(memory_space=pl.ANY)
    whole = pl.BlockSpec(memory_space=pltpu.VMEM)
    weight = jax.ShapeDtypeStruct((rows, channels), f32)
    gradient, table = pl.pallas_call(
        functools.partial(fused_kernel, sizes),
        out_shape=(weight, jax.ShapeDtypeStruct((2, n // 2, seq_chip, 128), f32)),
        in_specs=[hbm] * 6 + [whole],
        out_specs=(hbm, whole),
        scratch_shapes=[
            vmem((2, tokens_own, depth), bf),
            vmem((2, tokens_own, half), bf),
            vmem((half, 2 * tokens_own), bf),
            vmem((4, 2, rows, half), f32),
            vmem((4, 2, low, block), bf),
            vmem((4, 2, low, block), bf),
            vmem((4, 2, low, block), f32),
            vmem((4, 2, low, block), bf),
            vmem((4, 2, low, block), bf),
            vmem((4, 2, low, block), f32),
            vmem((4, low, block), bf),
            vmem((4, low, block), bf),
            vmem((4, low, block), bf),
            vmem((4, low, block), bf),
            vmem((3, half, block), bf),
            vmem((3, half, block), bf),
            vmem((half, block), f32),
            vmem((2, rows, half), f32),
            vmem((2, depth, half), bf),
            vmem((2, 4, tokens_own // 2, half), f32),
            vmem((2, n // 2, seq_chip, 128), f32),
            dma((18,)),
            dma((18,)),
            dma((18,)),
            dma((5, 4)),
            dma((5, 4)),
            dma((1,)),
            dma((1,)),
            dma((2, 2, 4)),
            dma((2, 4)),
            dma((2, 3)),
            dma((2, 4)),
            dma((4, 2)),
            dma((4, 2)),
            dma((4, 2, 2)),
            dma((4, 2, 2)),
            dma((10,)),
            dma((10,)),
        ],
        compiler_params=pltpu.CompilerParams(
            collective_id=0, has_side_effects=True, vmem_limit_bytes=56 * 1024 * 1024
        ),
    )(
        tokens,
        cotangent,
        policy,
        anchor,
        moment,
        second,
        readout.reshape(2, 1, half),
    )
    smem = pl.BlockSpec(memory_space=pltpu.SMEM)
    policy_next, anchor_next, moment_next, second_next, pair_loss = pl.pallas_call(
        finish_kernel,
        out_shape=(weight,) * 4 + (jax.ShapeDtypeStruct(noisy_flags.shape, f32),),
        in_specs=[whole] * 6 + [smem] * 2,
        out_specs=(whole,) * 4 + (smem,),
    )(
        gradient,
        policy,
        anchor,
        moment,
        second,
        table.reshape(2, n // 2 * seq_chip, 128),
        pair_index,
        noisy_flags,
    )
    return (policy_next, anchor_next, moment_next, second_next, pair_loss)


def solution(mesh):
    placed = (
        P(("rep", "fsdp"), None),
        P(("rep", "fsdp"), None),
        P("fsdp", None),
        P("fsdp", None),
        P("fsdp", None),
        P("fsdp", None),
        P(),
        P(("rep", "fsdp"), None),
        P(("rep", "fsdp")),
    )
    n = mesh.shape["fsdp"]
    body = shards
    if mesh.shape["rep"] == 1 and n // 8 == len(STEP_ORDER):
        body = functools.partial(fused_shards, n)
    return jax.shard_map(
        body,
        mesh=mesh,
        in_specs=placed,
        out_specs=(
            P("fsdp", None),
            P("fsdp", None),
            P("fsdp", None),
            P("fsdp", None),
            P(("rep", "fsdp")),
        ),
        check_vma=False,
    )
```

```python
import functools
import itertools
import jax
import jax.numpy as jnp
from jax import lax
from jax.experimental import pallas as pl
from jax.experimental.pallas import tpu as pltpu
from jax.sharding import PartitionSpec as P

LEN = 192


beta_one = 0.9
beta_two = 0.95
step_count = 20
learn_rate = 0.003
adam_epsilon = 1e-08
blend_rate = 0.6
smoothing = 0.1


def adam_update(gradient, policy, anchor, moment, second):
    moment_new = beta_one * moment + (1.0 - beta_one) * gradient
    second_new = beta_two * second + (1.0 - beta_two) * gradient * gradient
    correct_one = 1.0 - beta_one**step_count
    correct_two = 1.0 - beta_two**step_count
    policy_new = policy - learn_rate * (moment_new / correct_one) / (
        jnp.sqrt(second_new / correct_two) + adam_epsilon
    )
    anchor_new = blend_rate * policy_new + (1.0 - blend_rate) * anchor
    return (policy_new, anchor_new, moment_new, second_new)


def token_scores(values, readout):
    return jnp.sum(jax.nn.log_sigmoid(values * readout[None, :]), axis=1)


def sequence_margin(policy_values, anchor_values, readout, sequence_length):
    token_gap = token_scores(policy_values, readout) - token_scores(anchor_values, readout)
    return jnp.mean(token_gap.reshape(-1, sequence_length), axis=1)


def pair_losses(margins, pair_index, noisy_flags):
    sequence_index = jnp.arange(margins.shape[0], dtype=jnp.int32)
    chosen = jnp.sum(
        jnp.where(pair_index[:, 0:1] == sequence_index[None, :], margins[None, :], 0.0), axis=1
    )
    rejected = jnp.sum(
        jnp.where(pair_index[:, 1:2] == sequence_index[None, :], margins[None, :], 0.0), axis=1
    )
    margin_gap = chosen - rejected
    logit_value = jnp.where(noisy_flags == 1, -margin_gap, margin_gap)
    return -(1.0 - smoothing) * jax.nn.log_sigmoid(logit_value) - smoothing * jax.nn.log_sigmoid(
        -logit_value
    )


def shards(tokens, cotangent, policy, anchor, moment, second, readout, pair_index, noisy_flags):
    part_sum = lax.psum_scatter(
        lax.dot_general(
            tokens, cotangent, (((0,), (0,)), ((), ())), preferred_element_type=jnp.float32
        ),
        "fsdp",
        scatter_dimension=0,
        tiled=True,
    )
    gradient = lax.psum(part_sum.astype(jnp.bfloat16), "rep").astype(jnp.float32)
    policy_next, anchor_next, moment_next, second_next = adam_update(
        gradient, policy, anchor, moment, second
    )
    policy_half = policy_next.astype(jnp.bfloat16)
    anchor_half = anchor_next.astype(jnp.bfloat16)
    policy_whole = lax.all_gather(policy_half, "fsdp", axis=0, tiled=True)
    anchor_whole = lax.all_gather(anchor_half, "fsdp", axis=0, tiled=True)
    policy_values = jnp.dot(tokens, policy_whole, preferred_element_type=jnp.float32)
    anchor_values = jnp.dot(tokens, anchor_whole, preferred_element_type=jnp.float32)
    margins_own = sequence_margin(policy_values, anchor_values, readout, LEN)
    all_margins = lax.all_gather(margins_own, ("rep", "fsdp"), axis=0, tiled=True)
    pair_loss = pair_losses(all_margins, pair_index, noisy_flags)
    return (policy_next, anchor_next, moment_next, second_next, pair_loss)


STEP_ORDER = (2, 1, 3, 0)
MESH_ID = pl.DeviceIdType.MESH


def fused_kernel(
    sizes,
    tokens,
    cotangent,
    policy,
    anchor,
    moment,
    second,
    readout,
    gradient_out,
    margin_out,
    tok,
    cot,
    cot_t,
    par,
    send_a1,
    recv_a1,
    keep_a,
    send_b1,
    recv_b1,
    keep_b,
    send_a2,
    recv_a2,
    send_b2,
    recv_b2,
    send_z,
    recv_z,
    grad_own,
    result,
    weights,
    acc,
    table,
    local_sem,
    swap_send,
    swap_recv,
    rs_send,
    rs_recv,
    out_send,
    out_recv,
    z_send,
    z_recv,
    g2_send,
    g2_recv,
    g3_send,
    g3_recv,
    m_send,
    m_recv,
):
    n, rows, tokens_own, half, depth, seq_own = sizes
    block = 2 * rows
    span = 4 * block
    low = half // 2
    me = lax.axis_index("fsdp")
    core = me % 2
    px = (me // 2) % 2
    py = (me // 4) % 2
    pz = me // 8
    chip = me // 2
    mate = me + 1 - 2 * core
    x_mate = me + 2 - 4 * px
    y_mate = me + 4 - 8 * py

    def z_mate(shift):
        return (me + 8 * shift) % n

    def remote(src, dst, send_sem, recv_sem, device):
        return pltpu.make_async_remote_copy(
            src_ref=src,
            dst_ref=dst,
            send_sem=send_sem,
            recv_sem=recv_sem,
            device_id={"fsdp": device},
            device_id_type=MESH_ID,
        )

    barrier = pltpu.get_barrier_semaphore()
    plane = [
        me + dc * (1 - 2 * core) + dx * (2 - 4 * px) + dy * (4 - 8 * py)
        for dc, dx, dy in itertools.product((0, 1), repeat=3)
    ][1:]
    others = plane + [z_mate(s) for s in (1, 2, 3)]
    for other in others:
        pl.semaphore_signal(barrier, inc=1, device_id={"fsdp": other}, device_id_type=MESH_ID)

    mine = pl.ds(pl.multiple_of(core * half, half), half)
    theirs = pl.ds(pl.multiple_of((1 - core) * half, half), half)
    params = (policy, anchor, moment, second)

    pair = 2 * block

    def columns(s, dy):
        start = ((pz + s) % 4) * span + ((py + dy) % 2) * pair
        return pl.ds(pl.multiple_of(start, pair), pair)

    pieces = [(s, dy) for s in STEP_ORDER for dy in (1, 0)]

    cot_local = pltpu.make_async_copy(cotangent.at[:, mine], cot.at[core], local_sem.at[4])
    cot_local.start()
    tok_local = {}
    for i, (s, dy) in enumerate(pieces):
        tok_local[s, dy] = pltpu.make_async_copy(
            tokens.at[:, columns(s, dy)], tok.at[core, :, columns(s, dy)], local_sem.at[10 + i]
        )
        tok_local[s, dy].start()
    par_local = []
    for a in range(4):
        copy = pltpu.make_async_copy(params[a].at[:, mine], par.at[a, core], local_sem.at[5 + a])
        copy.start()
        par_local.append(copy)

    pl.semaphore_wait(barrier, len(others))

    sends = []
    cot_swap = remote(cotangent.at[:, theirs], cot.at[core], swap_send.at[4], swap_recv.at[4], mate)
    cot_swap.start()
    sends.append(cot_swap)
    tok_swap = {}
    for i, (s, dy) in enumerate(pieces):
        tok_swap[s, dy] = remote(
            tokens.at[:, columns(s, dy)],
            tok.at[core, :, columns(s, dy)],
            swap_send.at[10 + i],
            swap_recv.at[10 + i],
            mate,
        )
        tok_swap[s, dy].start()
        sends.append(tok_swap[s, dy])
    par_swap = []
    for a in range(4):
        copy = remote(
            params[a].at[:, theirs], par.at[a, core], swap_send.at[5 + a], swap_recv.at[5 + a], mate
        )
        copy.start()
        par_swap.append(copy)
        sends.append(copy)

    cot_local.wait()
    cot_swap.wait_recv()
    for r in range(2):
        cot_t[:, r * tokens_own : (r + 1) * tokens_own] = (
            cot[r].astype(jnp.float32).T.astype(jnp.bfloat16)
        )

    def first(s, dy):
        tok_local[s, dy].wait()
        tok_swap[s, dy].wait_recv()

    def block_gradient(s, dy, dx):
        target = ((pz + s) % 4) * 4 + ((py + dy) % 2) * 2 + (px + dx) % 2
        where = pl.ds(pl.multiple_of(target * block, block), block)
        total = jnp.dot(
            cot_t[:, :tokens_own], tok[0, :, where], preferred_element_type=jnp.float32
        )
        total += jnp.dot(
            cot_t[:, tokens_own:], tok[1, :, where], preferred_element_type=jnp.float32
        )
        if dx == 1:
            send_a1[s, dy] = total[:low].astype(jnp.bfloat16)
        else:
            keep_a[s, dy] = total[:low]
        if dy == 1:
            send_b1[s, dx] = total[low:].astype(jnp.bfloat16)
        else:
            keep_b[s, dx] = total[low:]

    hops = {}

    def hop(name, s, slot, src, dst, device):
        copy = remote(src, dst, rs_send.at[slot, s], rs_recv.at[slot, s], device)
        copy.start()
        hops[name, s] = copy
        sends.append(copy)

    def stage_one(s):
        first(s, 1)
        block_gradient(s, 1, 1)
        block_gradient(s, 1, 0)
        hop("b1", s, 1, send_b1.at[s], recv_b1.at[s], y_mate)
        first(s, 0)
        block_gradient(s, 0, 1)
        hop("a1", s, 0, send_a1.at[s], recv_a1.at[s], x_mate)
        block_gradient(s, 0, 0)

    def stage_two(s):
        hops["a1", s].wait_recv()
        send_a2[s] = (keep_a[s, 1] + recv_a1[s, 1].astype(jnp.float32)).astype(jnp.bfloat16)
        hop("a2", s, 2, send_a2.at[s], recv_a2.at[s], y_mate)
        hops["b1", s].wait_recv()
        send_b2[s] = (keep_b[s, 1] + recv_b1[s, 1].astype(jnp.float32)).astype(jnp.bfloat16)
        hop("b2", s, 3, send_b2.at[s], recv_b2.at[s], x_mate)

    def stage_three(s):
        hops["a2", s].wait_recv()
        total_a = keep_a[s, 0] + recv_a1[s, 0].astype(jnp.float32) + recv_a2[s].astype(jnp.float32)
        hops["b2", s].wait_recv()
        total_b = keep_b[s, 0] + recv_b1[s, 0].astype(jnp.float32) + recv_b2[s].astype(jnp.float32)
        if s == 0:
            grad_own[:low] = total_a
            grad_own[low:] = total_b
        else:
            send_z[s - 1, :low] = total_a.astype(jnp.bfloat16)
            send_z[s - 1, low:] = total_b.astype(jnp.bfloat16)
            hop("z", s, 4, send_z.at[s - 1], recv_z.at[s - 1], z_mate(s))

    for i in range(len(STEP_ORDER) + 2):
        if i < len(STEP_ORDER):
            stage_one(STEP_ORDER[i])
        if 1 <= i <= len(STEP_ORDER):
            stage_two(STEP_ORDER[i - 1])
        if i >= 2:
            stage_three(STEP_ORDER[i - 2])

    for a in range(4):
        par_local[a].wait()
        par_swap[a].wait_recv()
    for s in STEP_ORDER[:3]:
        hops["z", s].wait_recv()
    gradient = grad_own[...]
    for s in range(3):
        gradient += recv_z[s].astype(jnp.float32)
    gradient = gradient.T
    home = chip * block
    for r in range(2):
        updated = adam_update(
            gradient[r * rows : (r + 1) * rows], par[0, r], par[1, r], par[2, r], par[3, r]
        )
        result[r] = gradient[r * rows : (r + 1) * rows]
        for m in range(2):
            weights[m, pl.ds(pl.multiple_of(home + r * rows, rows), rows), :] = updated[m].astype(
                jnp.bfloat16
            )

    top = pz // 2
    near = pz + top * (3 - 2 * pz)

    def source(t):
        there = (near, 1 - near, 2, 3)[t]
        return there + top * (3 - 2 * there)

    def part(m, k):
        return weights.at[m, pl.ds(pl.multiple_of(k * block, block), block), :]

    def z_copy(m, zz, way):
        ref = part(m, zz * 4 + py * 2 + px)
        device = z_mate(1) if way == 0 else z_mate(3)
        return remote(ref, ref, z_send.at[way, m, zz], z_recv.at[m, zz], device)

    def z_forward(zz, act):
        @pl.when(jnp.logical_and(zz <= pz, pz < 3))
        def _():
            for m in range(2):
                act(z_copy(m, zz, 0))

        @pl.when(jnp.logical_and(zz >= pz, pz > 0))
        def _():
            for m in range(2):
                act(z_copy(m, zz, 1))

    gathers = {}

    def gather_two(t, zz):
        for m in range(2):
            ref = part(m, zz * 4 + py * 2 + px)
            device = y_mate if m == 0 else x_mate
            copy = remote(ref, ref, g2_send.at[t, m], g2_recv.at[t, m], device)
            copy.start()
            gathers[2, t, m] = copy
            sends.append(copy)

    def gather_three(t, zz, late, m):
        ky = (py + late) % 2 if m == 0 else py
        kx = px if m == 0 else (px + late) % 2
        ref = part(m, zz * 4 + ky * 2 + kx)
        device = x_mate if m == 0 else y_mate
        copy = remote(ref, ref, g3_send.at[t, late, m], g3_recv.at[t, late, m], device)
        copy.start()
        gathers[3, t, late, m] = copy
        sends.append(copy)

    tile = tokens_own
    scale = readout[core]

    def score_sum(values):
        low_part = jnp.minimum(values, 0.0).reshape(LEN // 8, 8, half)
        factor = (1.0 + jnp.exp(-jnp.abs(values))).reshape(LEN // 8, 8, half)
        product = factor[0]
        for j in range(1, LEN // 8):
            product = product * factor[j]
        return jnp.sum(low_part, axis=0) - jnp.log(product)

    def arrived(t, late):
        for m in range(2):
            gathers[3, t, late, m].wait_recv()

    def compute(t, zz):
        where = pl.ds(pl.multiple_of(zz * span, span), span)

        @pl.loop(0, 2)
        def _(i):
            at = pl.ds(0, tile)
            lhs = tok[i, at, where]
            for m in range(2):
                value = jnp.dot(lhs, weights[m, where, :], preferred_element_type=jnp.float32)
                acc[m, i] = value if t == 0 else acc[m, i] + value

    def spot(zz, dy, dx):
        k = zz * 4 + ((py + dy) % 2) * 2 + (px + dx) % 2
        return pl.ds(pl.multiple_of(k * block, block), block)

    def compute_near(zz):
        @pl.loop(0, 2)
        def _(i):
            at = pl.ds(0, tile)
            for m in range(2):
                value = acc[m, i]
                for dy, dx in ((0, 0), (0, 1), (1, 0)):
                    where = spot(zz, dy, dx)
                    value += jnp.dot(
                        tok[i, at, where],
                        weights[m, where, :],
                        preferred_element_type=jnp.float32,
                    )
                acc[m, i] = value

    def compute_last(zz):
        where = spot(zz, 1, 1)

        @pl.loop(0, 2)
        def _(i):
            at = pl.ds(0, tile)
            lhs = tok[i, at, where]
            for m in range(2):
                value = jnp.dot(lhs, weights[m, where, :], preferred_element_type=jnp.float32)
                acc[m, i] = (value + acc[m, i]) * scale
            for j in range(tile // LEN):
                gap = score_sum(acc[0, i, j * LEN : (j + 1) * LEN]) - score_sum(
                    acc[1, i, j * LEN : (j + 1) * LEN]
                )
                gap = jnp.sum(gap, axis=0, keepdims=True)
                gap = jnp.sum(gap, axis=1, keepdims=True)
                table[core, chip, pl.ds(i * (tile // LEN) + j, 1), :] = jnp.broadcast_to(
                    gap * (1.0 / LEN), (1, 128)
                )

    waits = []
    for t in range(4):
        zz = source(t)
        if t > 0:
            for m in range(2):
                z_copy(m, zz, 0).wait_recv()
        z_forward(zz, lambda copy: copy.start())
        gather_two(t, zz)
        gather_three(t, zz, 0, 0)
        gather_three(t, zz, 0, 1)
        if t == 0:
            copy = pltpu.make_async_copy(result.at[core], gradient_out.at[:, mine], local_sem.at[9])
            copy.start()
            waits.append(copy)
            copy = remote(
                result.at[1 - core], gradient_out.at[:, mine], out_send.at[0], out_recv.at[0], mate
            )
            copy.start()
            waits.append(copy)
        for m in range(2):
            gathers[2, t, m].wait_recv()
            gather_three(t, zz, 1, m)
        if t > 0:
            arrived(t - 1, 0)
            arrived(t - 1, 1)
            compute(t - 1, source(t - 1))
    arrived(3, 0)
    compute_near(source(3))
    arrived(3, 1)
    compute_last(source(3))

    def table_copy(ref, slot, device):
        copy = remote(ref, ref, m_send.at[slot], m_recv.at[slot], device)
        copy.start()
        sends.append(copy)
        return copy

    near_copies = [
        table_copy(table.at[core, pl.ds(chip, 1)], i, device) for i, device in enumerate(plane)
    ]
    for copy in near_copies:
        copy.wait_recv()
    last = [
        table_copy(table.at[:, pl.ds(pz * 4, 4)], 6 + s, z_mate(s)) for s in (2, 1, 3)
    ]
    for copy in last:
        copy.wait_recv()
    for copy in waits:
        copy.wait()
    for copy in sends:
        copy.wait_send()
    for t in range(4):
        z_forward(source(t), lambda copy: copy.wait_send())
    margin_out[...] = table[...]


def finish_kernel(
    gradient,
    policy,
    anchor,
    moment,
    second,
    table,
    pair_index,
    noisy_flags,
    policy_out,
    anchor_out,
    moment_out,
    second_out,
    loss_out,
):
    updated = adam_update(gradient[...], policy[...], anchor[...], moment[...], second[...])
    for out, value in zip((policy_out, anchor_out, moment_out, second_out), updated):
        out[...] = value
    margins = table[0] + table[1]
    sequence = lax.broadcasted_iota(jnp.int32, margins.shape, 0)

    def margin_of(index):
        return jnp.sum(jnp.where(sequence == index, margins, 0.0), axis=0, keepdims=True)

    for p in range(noisy_flags.shape[0]):
        gap = margin_of(pair_index[p, 0]) - margin_of(pair_index[p, 1])
        gap = jnp.where(noisy_flags[p] == 1, -gap, gap)
        tail = jnp.log(1.0 + jnp.exp(-jnp.abs(gap)))
        loss = (1.0 - smoothing) * (tail - jnp.minimum(gap, 0.0)) + smoothing * (
            tail + jnp.maximum(gap, 0.0)
        )
        loss_out[p] = loss[0, 0]


def fused_shards(n, tokens, cotangent, policy, anchor, moment, second, readout, pair_index, noisy_flags):
    tokens_own, depth = tokens.shape
    rows, channels = policy.shape
    half = channels // 2
    block = 2 * rows
    low = half // 2
    seq_chip = 2 * tokens_own // LEN
    sizes = (n, rows, tokens_own, half, depth, seq_chip // 2)
    bf, f32 = jnp.bfloat16, jnp.float32
    vmem, dma = pltpu.VMEM, pltpu.SemaphoreType.DMA
    hbm = pl.BlockSpec(memory_space=pl.ANY)
    whole = pl.BlockSpec(memory_space=pltpu.VMEM)
    weight = jax.ShapeDtypeStruct((rows, channels), f32)
    gradient, table = pl.pallas_call(
        functools.partial(fused_kernel, sizes),
        out_shape=(weight, jax.ShapeDtypeStruct((2, n // 2, seq_chip, 128), f32)),
        in_specs=[hbm] * 6 + [whole],
        out_specs=(hbm, whole),
        scratch_shapes=[
            vmem((2, tokens_own, depth), bf),
            vmem((2, tokens_own, half), bf),
            vmem((half, 2 * tokens_own), bf),
            vmem((4, 2, rows, half), f32),
            vmem((4, 2, low, block), bf),
            vmem((4, 2, low, block), bf),
            vmem((4, 2, low, block), f32),
            vmem((4, 2, low, block), bf),
            vmem((4, 2, low, block), bf),
            vmem((4, 2, low, block), f32),
            vmem((4, low, block), bf),
            vmem((4, low, block), bf),
            vmem((4, low, block), bf),
            vmem((4, low, block), bf),
            vmem((3, half, block), bf),
            vmem((3, half, block), bf),
            vmem((half, block), f32),
            vmem((2, rows, half), f32),
            vmem((2, depth, half), bf),
            vmem((2, 2, tokens_own, half), f32),
            vmem((2, n // 2, seq_chip, 128), f32),
            dma((18,)),
            dma((18,)),
            dma((18,)),
            dma((5, 4)),
            dma((5, 4)),
            dma((1,)),
            dma((1,)),
            dma((2, 2, 4)),
            dma((2, 4)),
            dma((4, 2)),
            dma((4, 2)),
            dma((4, 2, 2)),
            dma((4, 2, 2)),
            dma((10,)),
            dma((10,)),
        ],
        compiler_params=pltpu.CompilerParams(
            collective_id=0, has_side_effects=True, vmem_limit_bytes=56 * 1024 * 1024
        ),
    )(
        tokens,
        cotangent,
        policy,
        anchor,
        moment,
        second,
        readout.reshape(2, 1, half),
    )
    smem = pl.BlockSpec(memory_space=pltpu.SMEM)
    policy_next, anchor_next, moment_next, second_next, pair_loss = pl.pallas_call(
        finish_kernel,
        out_shape=(weight,) * 4 + (jax.ShapeDtypeStruct(noisy_flags.shape, f32),),
        in_specs=[whole] * 6 + [smem] * 2,
        out_specs=(whole,) * 4 + (smem,),
    )(
        gradient,
        policy,
        anchor,
        moment,
        second,
        table.reshape(2, n // 2 * seq_chip, 128),
        pair_index,
        noisy_flags,
    )
    return (policy_next, anchor_next, moment_next, second_next, pair_loss)


def solution(mesh):
    placed = (
        P(("rep", "fsdp"), None),
        P(("rep", "fsdp"), None),
        P("fsdp", None),
        P("fsdp", None),
        P("fsdp", None),
        P("fsdp", None),
        P(),
        P(("rep", "fsdp"), None),
        P(("rep", "fsdp")),
    )
    n = mesh.shape["fsdp"]
    body = shards
    if mesh.shape["rep"] == 1 and n // 8 == len(STEP_ORDER):
        body = functools.partial(fused_shards, n)
    return jax.shard_map(
        body,
        mesh=mesh,
        in_specs=placed,
        out_specs=(
            P("fsdp", None),
            P("fsdp", None),
            P("fsdp", None),
            P("fsdp", None),
            P(("rep", "fsdp")),
        ),
        check_vma=False,
    )
```
